256 devices in a mesh: seq: 128 (over y, x_lo, z, core), mp: 2 (over x_hi).
Axes of the slice: x: 4 (x_hi: 2, x_lo: 2; x = x_hi * 2 + x_lo), y: 4, z: 8, core: 2. Of those that a mesh axis runs over, the one named last changes fastest.
Arguments:
- normed: bfloat16 [65536, 2048], P('seq', 'mp'), may hold values from -18 to 18
- router: bfloat16 [2048], replicated, may hold values from -0.125 to 0.125
- light_qkv: bfloat16 [3, 2048, 1024], P(None, None, 'mp'), may hold values from -0.125 to 0.125
- light_out: bfloat16 [1024, 2048], P('mp'), may hold values from -0.1875 to 0.1875
- heavy_qkv: bfloat16 [3, 2048, 1024], P(None, 'seq', 'mp'), may hold values from -0.125 to 0.125
- heavy_out: bfloat16 [1024, 2048], P('mp', 'seq'), may hold values from -0.1875 to 0.1875
- query_slots: int32 [128, 32], P('seq'), may hold values from 0 to 511, as said below
- query_count: int32 [128], P('seq'), may hold values from 1 to 32, 2048 in all
- key_slots: int32 [128, 32], P('seq'), may hold values from 0 to 511, as said below
- key_count: int32 [128], P('seq'), may hold values from 1 to 32, 2048 in all
Outputs:
- mixed: bfloat16 [65536, 2048], P('seq', 'mp')
The draws below stay inside these ranges and needn't reach their ends.
Inputs may be any that keep to these rules, and one draw needn't show every extreme that they name: `query_slots`: each row holds 32 distinct positions of one shard's 512 tokens; only the first query_count entries of a row are live. `key_slots`: each row holds 32 distinct positions of one shard's 512 tokens; only the first key_count entries of a row are live. `query_count`: the counts sum to 2048 and the largest is exactly 32. `key_count`: the counts sum to 2048 and the largest is exactly 32.
All inputs are finite; a program needn't handle non-finite values.
Results may differ from the reference program's by a relative error of at most 0.012.
Values may be sent and summed in bfloat16 or wider, within the bound.
No kernel may reach another device: no remote copies, remote signals or barrier semaphores. Data moves between devices by JAX's collectives and lax.ppermute only.
A program may use at most 128 MiB of HBM per device.

```python
import math
import jax
import jax.numpy as jnp
import numpy as np
from jax import lax

D = 2048
LHEADS = 16
HHEADS = 16
HEAD_DIM = 64
RADIUS = 64
TOK_DEV = 512
CAP = 32
SHARDS = 128
TOKENS = 65536


def draw_normed(key, part):
    base = jax.random.fold_in(jax.random.fold_in(key, 5), 0)
    values = jax.random.normal(base, (TOKENS, D), jnp.float32) * 1.75
    return jnp.clip(values, -7.0, 7.0).astype(jnp.bfloat16)


def slots_from(key, salt):
    shard_keys = jax.random.split(jax.random.fold_in(key, salt), SHARDS)

    def one_shard(shard_key):
        return jax.random.permutation(shard_key, TOK_DEV)[:CAP].astype(jnp.int32)
    return jax.vmap(one_shard)(shard_keys)


def draw_query_slots(key, part):
    return slots_from(key, 11)


def draw_key_slots(key, part):
    return slots_from(key, 23)


def block_scale(rng, extent, cuts, smallest, top_value):
    def one(position, blocks):
        heights = jax.random.uniform(jax.random.fold_in(jax.random.fold_in(rng, 6), position), (blocks,), jnp.float32, smallest / len(cuts), top_value / len(cuts))
        return jnp.repeat(jnp.exp(heights), extent[position] // blocks).reshape((-1,) + (1,) * (len(extent) - position - 1))

    gain = one(*cuts[0])
    for cut in cuts[1:]:
        gain = gain * one(*cut)
    return gain


def split_up(count, total, most, lean):
    weights = [(1 << 20) // math.isqrt(rank ** lean) + 1 for rank in range(2, count + 1)]
    spare, holding = total - most - (count - 1), [1] * (count - 1)
    while spare > 0:
        free = [i for i in range(count - 1) if holding[i] < most]
        mass, remaining = sum([weights[i] for i in free]), spare
        for i in free:
            more = min(most - holding[i], max(1, remaining * weights[i] // mass), spare)
            holding[i] = holding[i] + more
            spare = spare - more
    return np.array([most] + holding)


def uneven_parts(rng, count, total, bound, slope):
    if count == 2:
        one = jax.random.randint(rng, (), max(1, total - bound), min(bound, total - 1) + 1)
        return jnp.stack([one, total - one])
    lengths = jnp.asarray(split_up(count, total, bound, slope), jnp.int32)
    pairs = (count - 1) // 2
    donor, taker = lengths[1:1 + 2 * pairs:2], lengths[2:2 + 2 * pairs:2]
    room = jnp.minimum(donor - 1, bound - taker)
    moved = jax.random.randint(jax.random.fold_in(rng, 1), (pairs,), 0, 1 << 20) % (room + 1)
    lengths = lengths.at[1:1 + 2 * pairs:2].set(donor - moved).at[2:2 + 2 * pairs:2].set(taker + moved)
    return lengths[jax.random.permutation(jax.random.fold_in(rng, 2), count)]


def bell_draw(rng, dims, deviation, limit, shards=(), held_as=jnp.bfloat16):
    drawn = jax.random.normal(rng, dims, jnp.float32) * deviation
    if len(shards) > 0:
        drawn = block_scale(rng, dims, shards, -0.22, 0.18) * drawn
    return jnp.clip(drawn, min=-limit, max=limit).astype(held_as)


def setup_inputs(seed: int = 0) -> dict:
    keys = jax.random.split(jax.random.key(seed), 11)
    return {
        "normed": draw_normed(jax.random.fold_in(keys[10], 71), 0),
        "router": bell_draw(keys[1], (D,), D ** -0.5, 0.125),
        "light_qkv": bell_draw(keys[2], (3, D, LHEADS * HEAD_DIM), D ** -0.5, 0.125, ((2, 2),)),
        "light_out": bell_draw(keys[3], (LHEADS * HEAD_DIM, D), (LHEADS * HEAD_DIM) ** -0.5, 0.1875, ((0, 2),)),
        "heavy_qkv": bell_draw(keys[4], (3, D, HHEADS * HEAD_DIM), D ** -0.5, 0.125, ((1, 128), (2, 2))),
        "heavy_out": bell_draw(keys[5], (HHEADS * HEAD_DIM, D), (HHEADS * HEAD_DIM) ** -0.5, 0.1875, ((0, 2), (1, 128))),
        "query_slots": draw_query_slots(jax.random.fold_in(keys[10], 71), 0),
        "query_count": uneven_parts(keys[7], SHARDS, SHARDS * CAP // 2, CAP, 2).astype(jnp.int32),
        "key_slots": draw_key_slots(jax.random.fold_in(keys[10], 71), 0),
        "key_count": uneven_parts(keys[9], SHARDS, SHARDS * CAP // 2, CAP, 2).astype(jnp.int32),
    }


NEG = -1.0e30


def mix_heads(queries, key_rows, value_rows, allowed):
    length = queries.shape[0]
    head_count = queries.shape[1] // HEAD_DIM
    query_heads = queries.astype(jnp.float32).reshape(length, head_count, HEAD_DIM)
    key_heads = key_rows.astype(jnp.float32).reshape(key_rows.shape[0], head_count, HEAD_DIM)
    value_heads = value_rows.astype(jnp.float32).reshape(value_rows.shape[0], head_count, HEAD_DIM)
    scores = jnp.einsum("qhe,khe->hqk", query_heads, key_heads) * (HEAD_DIM ** -0.5)
    scores = jnp.where(allowed[None], scores, NEG)
    row_peak = jnp.max(scores, axis=2, keepdims=True)
    weights = jnp.where(allowed[None], jnp.exp(scores - row_peak), 0.0)
    row_total = jnp.sum(weights, axis=2)
    rounded = weights.astype(jnp.bfloat16).astype(jnp.float32)
    blended = jnp.einsum("hqk,khe->qhe", rounded, value_heads) / jnp.transpose(row_total)[:, :, None]
    return blended.reshape(length, head_count * HEAD_DIM).astype(jnp.bfloat16)


def reference(normed, router, light_qkv, light_out, heavy_qkv, heavy_out, query_slots, query_count, key_slots, key_count):
    block_rows = min(512, TOK_DEV)
    light_q = jnp.dot(normed, light_qkv[0], preferred_element_type=jnp.float32).astype(jnp.bfloat16)
    light_k = jnp.dot(normed, light_qkv[1], preferred_element_type=jnp.float32).astype(jnp.bfloat16)
    light_v = jnp.dot(normed, light_qkv[2], preferred_element_type=jnp.float32).astype(jnp.bfloat16)
    padding = jnp.zeros((RADIUS, light_k.shape[1]), jnp.bfloat16)
    keys_padded = jnp.concatenate([padding, light_k, padding], 0)
    values_padded = jnp.concatenate([padding, light_v, padding], 0)

    def light_block(offset):
        queries = lax.dynamic_slice_in_dim(light_q, offset, block_rows, 0)
        key_rows = lax.dynamic_slice_in_dim(keys_padded, offset, block_rows + 2 * RADIUS, 0)
        value_rows = lax.dynamic_slice_in_dim(values_padded, offset, block_rows + 2 * RADIUS, 0)
        query_pos = offset + jnp.arange(block_rows, dtype=jnp.int32)
        key_pos = offset - RADIUS + jnp.arange(block_rows + 2 * RADIUS, dtype=jnp.int32)
        distance = jnp.abs(query_pos[:, None] - key_pos[None, :])
        allowed = (distance <= RADIUS) & (key_pos[None, :] >= 0) & (key_pos[None, :] < TOKENS)
        return mix_heads(queries, key_rows, value_rows, allowed)

    offsets = jnp.arange(TOKENS // block_rows, dtype=jnp.int32) * block_rows
    context = lax.map(light_block, offsets).reshape(TOKENS, light_q.shape[1])

    shard_base = (jnp.arange(SHARDS, dtype=jnp.int32) * TOK_DEV)[:, None]
    slot_range = jnp.arange(CAP, dtype=jnp.int32)[None, :]
    query_rows = (query_slots + shard_base).reshape(-1)
    key_token_rows = (key_slots + shard_base).reshape(-1)
    query_live = (slot_range < query_count[:, None]).reshape(-1)
    key_live = (slot_range < key_count[:, None]).reshape(-1)
    query_inputs = normed[query_rows]
    key_inputs = normed[key_token_rows]
    heavy_q = jnp.dot(query_inputs, heavy_qkv[0], preferred_element_type=jnp.float32).astype(jnp.bfloat16)
    heavy_k = jnp.dot(key_inputs, heavy_qkv[1], preferred_element_type=jnp.float32).astype(jnp.bfloat16)
    heavy_v = jnp.dot(key_inputs, heavy_qkv[2], preferred_element_type=jnp.float32).astype(jnp.bfloat16)
    slot_total = SHARDS * CAP
    heavy_block = min(512, slot_total)
    allowed_keys = key_live[None, :]

    def heavy_part(offset):
        queries = lax.dynamic_slice_in_dim(heavy_q, offset, heavy_block, 0)
        return mix_heads(queries, heavy_k, heavy_v, allowed_keys)

    heavy_offsets = jnp.arange(slot_total // heavy_block, dtype=jnp.int32) * heavy_block
    heavy_context = lax.map(heavy_part, heavy_offsets).reshape(slot_total, heavy_q.shape[1])
    gate = jax.nn.sigmoid(jnp.dot(query_inputs, router, preferred_element_type=jnp.float32))
    gate = jnp.where(query_live, gate, 0.0)
    heavy_rows = jnp.dot(heavy_context, heavy_out, preferred_element_type=jnp.float32) * gate[:, None]
    combined = jnp.dot(context, light_out, preferred_element_type=jnp.float32)
    combined = combined.at[query_rows].add(heavy_rows)
    return combined.astype(jnp.bfloat16)
```

```python
import functools

import jax
import jax.numpy as jnp
from jax import lax
from jax.experimental import pallas as pl
from jax.experimental.pallas import tpu as pltpu
from jax.sharding import Mesh
from jax.sharding import PartitionSpec as P

HEAD_DIM = 64
RADIUS = 64
NEG = -1e30
SEQ = ("y", "xl", "z", "c")
GROUP = ("y", "xl")


NT = (((1,), (1,)), ((), ()))


def spec(shape, index):
    return pl.BlockSpec(shape, index)


def project_own_kernel(pos, x_ref, w_ref, out_ref):
    out_ref[0] = jnp.dot(x_ref[...], w_ref[0], preferred_element_type=jnp.float32)


def project_own(pos, x, w):
    rows, half = x.shape
    cols = w.shape[2]
    return pl.pallas_call(
        project_own_kernel,
        out_shape=jax.ShapeDtypeStruct((3, rows, cols), jnp.float32),
        grid_spec=pltpu.PrefetchScalarGridSpec(
            num_scalar_prefetch=1,
            grid=(3,),
            in_specs=[
                spec((rows, half), lambda j, p: (0, 0)),
                spec((1, half, cols), lambda j, p: (j, p[1], 0)),
            ],
            out_specs=spec((1, rows, cols), lambda j, p: (j, 0, 0)),
        ),
        name="light_project_own",
    )(pos, x, w)


def project_add_kernel(pos, x_ref, w_ref, part_ref, out_ref):
    total = jnp.dot(x_ref[...], w_ref[0], preferred_element_type=jnp.float32) + part_ref[0]
    out_ref[0] = total.astype(jnp.bfloat16)


def project_add(pos, x, w, part, first, count):
    rows, half = x.shape
    cols = w.shape[2]
    return pl.pallas_call(
        project_add_kernel,
        out_shape=jax.ShapeDtypeStruct((count, rows, cols), jnp.bfloat16),
        grid_spec=pltpu.PrefetchScalarGridSpec(
            num_scalar_prefetch=1,
            grid=(count,),
            in_specs=[
                spec((rows, half), lambda j, p: (0, 0)),
                spec((1, half, cols), lambda j, p: (j + first, 1 - p[1], 0)),
                spec((1, rows, cols), lambda j, p: (j + first, 0, 0)),
            ],
            out_specs=spec((1, rows, cols), lambda j, p: (j, 0, 0)),
        ),
        name="light_project_add",
    )(pos, x, w, part)


def light_kernel(pos, q_ref, kv_ref, left_ref, right_ref, own_w_ref, other_w_ref, own_ref, other_ref, pad_ref, *, tokens):
    step = pl.program_id(0)
    block = q_ref.shape[1]
    length = kv_ref.shape[1]
    width = q_ref.shape[2]
    span = block + 2 * RADIUS

    @pl.when(step == 0)
    def _():
        pad_ref[:, 0:RADIUS, :] = left_ref[...]
        pad_ref[:, RADIUS : RADIUS + length, :] = kv_ref[...]
        pad_ref[:, RADIUS + length :, :] = right_ref[...]

    start = pl.multiple_of(step * block, block)
    row = lax.broadcasted_iota(jnp.int32, (block, span), 0)
    col = lax.broadcasted_iota(jnp.int32, (block, span), 1)
    key = pos[0] * length + step * block - RADIUS + col
    allowed = (col >= row) & (col - row <= 2 * RADIUS) & (key >= 0) & (key < tokens)
    bias = jnp.where(allowed, 0.0, NEG)
    bias = jnp.concatenate([bias, bias], axis=0)
    lane = lax.broadcasted_iota(jnp.int32, (block, 2 * HEAD_DIM), 1)
    first = lane < HEAD_DIM
    pieces = []
    for pair in range(width // (2 * HEAD_DIM)):
        lanes = slice(pair * 2 * HEAD_DIM, (pair + 1) * 2 * HEAD_DIM)
        q = q_ref[0, :, lanes]
        k = pad_ref[0, pl.ds(start, span), lanes]
        v = pad_ref[1, pl.ds(start, span), lanes]
        zero = jnp.zeros_like(q)
        both = jnp.concatenate([jnp.where(first, q, zero), jnp.where(first, zero, q)], axis=0)
        scores = lax.dot_general(both, k, NT, preferred_element_type=jnp.float32)
        scores = scores * (HEAD_DIM ** -0.5) + bias
        peak = jnp.max(scores, axis=1, keepdims=True)
        weights = jnp.exp(scores - peak)
        total = jnp.sum(weights, axis=1, keepdims=True)
        blended = jnp.dot(weights.astype(jnp.bfloat16), v, preferred_element_type=jnp.float32) / total
        pieces.append(jnp.where(first, blended[:block], blended[block:]).astype(jnp.bfloat16))
    context = jnp.concatenate(pieces, axis=1)
    other_ref[...] = jnp.dot(context, other_w_ref[...], preferred_element_type=jnp.float32).astype(jnp.bfloat16)
    own_ref[...] = jnp.dot(context, own_w_ref[...], preferred_element_type=jnp.float32)


def light_attention(pos, q, kv, left, right, w, tokens):
    rows, width = q.shape[1:]
    half = w.shape[1] // 2
    block = 128
    return pl.pallas_call(
        functools.partial(light_kernel, tokens=tokens),
        out_shape=(
            jax.ShapeDtypeStruct((rows, half), jnp.float32),
            jax.ShapeDtypeStruct((rows, half), jnp.bfloat16),
        ),
        grid_spec=pltpu.PrefetchScalarGridSpec(
            num_scalar_prefetch=1,
            grid=(rows // block,),
            in_specs=[
                spec((1, block, width), lambda b, p: (0, b, 0)),
                spec((2, rows, width), lambda b, p: (0, 0, 0)),
                spec((2, RADIUS, width), lambda b, p: (0, 0, 0)),
                spec((2, RADIUS, width), lambda b, p: (0, 0, 0)),
                spec((width, half), lambda b, p: (0, p[1])),
                spec((width, half), lambda b, p: (0, 1 - p[1])),
            ],
            out_specs=(
                spec((block, half), lambda b, p: (b, 0)),
                spec((block, half), lambda b, p: (b, 0)),
            ),
            scratch_shapes=[pltpu.VMEM((2, rows + 2 * RADIUS, width), jnp.bfloat16)],
        ),
        name="light_attention",
    )(pos, q, kv, left, right, w, w)


def pack_heads_kernel(count, qkv_ref, out_w_ref, packed_ref):
    depth = qkv_ref.shape[1]
    heads = qkv_ref.shape[2] // HEAD_DIM
    row = lax.broadcasted_iota(jnp.int32, (depth, depth), 0)
    col = lax.broadcasted_iota(jnp.int32, (depth, depth), 1)
    eye = jnp.where(row == col, 1.0, 0.0).astype(jnp.bfloat16)
    turned = lax.dot_general(eye, out_w_ref[...], NT, preferred_element_type=jnp.float32).astype(jnp.bfloat16)
    marks = jnp.full((packed_ref.shape[1] - depth, packed_ref.shape[2]), count[0], jnp.int32)
    marks = marks.astype(jnp.float32).astype(jnp.bfloat16)
    for h in range(heads):
        lanes = slice(h * HEAD_DIM, (h + 1) * HEAD_DIM)
        piece = jnp.concatenate([qkv_ref[0, :, lanes], turned[:, lanes], qkv_ref[1, :, lanes], qkv_ref[2, :, lanes]], axis=1)
        for side in range(2):
            packed_ref[2 * h + side, 0:depth, :] = piece
            packed_ref[2 * h + side, depth:, :] = marks


def pack_heads(count, qkv, out_w):
    depth = qkv.shape[1]
    heads = qkv.shape[2] // HEAD_DIM
    return pl.pallas_call(
        pack_heads_kernel,
        out_shape=jax.ShapeDtypeStruct((2 * heads, depth + 8, 4 * HEAD_DIM), jnp.bfloat16),
        grid_spec=pltpu.PrefetchScalarGridSpec(
            num_scalar_prefetch=1,
            grid=(1,),
            in_specs=[spec(qkv.shape, lambda i, p: (0, 0, 0)), spec(out_w.shape, lambda i, p: (0, 0))],
            out_specs=spec((2 * heads, depth + 8, 4 * HEAD_DIM), lambda i, p: (0, 0, 0)),
        ),
        name="pack_heads",
    )(count, qkv, out_w)


def pack_copies_kernel(pos, in_ref, out_ref, *, depth):
    side = pos[1]
    copies = out_ref.shape[0]
    group = in_ref.shape[0] // 2
    lane = lax.broadcasted_iota(jnp.int32, (depth, 4 * HEAD_DIM), 1)
    from_out = (lane >= HEAD_DIM) & (lane < 2 * HEAD_DIM)
    marks = []
    for i in range(group):
        qkv = in_ref[side * group + i, 0:depth, :]
        out_w = in_ref[2 * i + side, 0:depth, :]
        tile = jnp.where(from_out, out_w, qkv)
        marks.append(in_ref[2 * i + side, depth : depth + 1, :])
        for t in range(copies):
            out_ref[t, i * depth : (i + 1) * depth, :] = tile
    marks = jnp.concatenate(marks, axis=0)
    for t in range(copies):
        out_ref[t, group * depth :, :] = marks


def pack_copies(pos, sliced, copies):
    group = sliced.shape[0] // 2
    depth = sliced.shape[1] - 8
    shape = (copies, group * depth + group, 4 * HEAD_DIM)
    return pl.pallas_call(
        functools.partial(pack_copies_kernel, depth=depth),
        out_shape=jax.ShapeDtypeStruct(shape, jnp.bfloat16),
        grid_spec=pltpu.PrefetchScalarGridSpec(
            num_scalar_prefetch=1,
            grid=(1,),
            in_specs=[spec(sliced.shape, lambda i, p: (0, 0, 0))],
            out_specs=spec(shape, lambda i, p: (0, 0, 0)),
        ),
        name="pack_copies",
    )(pos, sliced)


def heavy_project_kernel(pos, mine_ref, theirs_ref, r0, r1, r2, r3, own_ref, other_ref, w_ref, *, depth, capacity):
    side, core, y, xl = pos[1], pos[2], pos[3], pos[4]
    z_size = mine_ref.shape[0]
    for y_half in range(2):
        for x in range(2):
            for m in range(2):
                i = (y_half * 2 + x) * 2 + m
                for z in range(z_size):
                    base = ((y_half * 2 + x) * z_size + z) * 2
                    w_ref[m, pl.ds(pl.multiple_of((base + core) * depth, depth), depth), :] = mine_ref[
                        z, i * depth : (i + 1) * depth, :
                    ]
                    w_ref[m, pl.ds(pl.multiple_of((base + 1 - core) * depth, depth), depth), :] = theirs_ref[
                        z, i * depth : (i + 1) * depth, :
                    ]
    lane = lax.broadcasted_iota(jnp.int32, (capacity, 2 * HEAD_DIM), 1)
    keep = lane < HEAD_DIM
    for target, w in ((other_ref, w_ref[1 - side]), (own_ref, w_ref[side])):
        for d, piece in enumerate((r0, r1, r2, r3)):
            rows = piece[...].reshape(4 * capacity, piece.shape[2])
            result = jnp.dot(rows, w, preferred_element_type=jnp.float32)
            source_y = lax.rem(y - d + 4, 4)
            for which in range(2):
                source = source_y * 2 + (xl if which == 0 else 1 - xl)
                top = which * 2 * capacity
                query = jnp.where(keep, result[top : top + capacity, : 2 * HEAD_DIM], 0.0)
                keys = result[top + capacity : top + 2 * capacity, 2 * HEAD_DIM :]
                value = jnp.concatenate([query, keys], axis=1)
                target[pl.ds(pl.multiple_of(source * capacity, capacity), capacity), :] = value.astype(target.dtype)


def heavy_project(pos, mine, theirs, pieces, depth):
    capacity = pieces[0].shape[1] // 2
    half = pieces[0].shape[2]
    slots = 8 * capacity
    whole3 = lambda i, p: (0, 0, 0)
    return pl.pallas_call(
        functools.partial(heavy_project_kernel, depth=depth, capacity=capacity),
        out_shape=(
            jax.ShapeDtypeStruct((slots, 4 * HEAD_DIM), jnp.float32),
            jax.ShapeDtypeStruct((slots, 4 * HEAD_DIM), jnp.bfloat16),
        ),
        grid_spec=pltpu.PrefetchScalarGridSpec(
            num_scalar_prefetch=1,
            grid=(1,),
            in_specs=[spec(mine.shape, whole3), spec(theirs.shape, whole3)] + [spec(p.shape, whole3) for p in pieces],
            out_specs=(
                spec((slots, 4 * HEAD_DIM), lambda i, p: (0, 0)),
                spec((slots, 4 * HEAD_DIM), lambda i, p: (0, 0)),
            ),
            scratch_shapes=[pltpu.VMEM((2, half, 4 * HEAD_DIM), jnp.bfloat16)],
        ),
        name="heavy_project",
    )(pos, mine, theirs, *pieces)


def finish_kernel(own_ref, arrived_ref, query_ref, copies_ref):
    total = (own_ref[...] + arrived_ref[...].astype(jnp.float32)).astype(jnp.bfloat16)
    query_ref[...] = total[:, : 2 * HEAD_DIM]
    for t in range(copies_ref.shape[0]):
        copies_ref[t] = total[:, 2 * HEAD_DIM :]


def finish(own, arrived, copies):
    slots = own.shape[0]
    return pl.pallas_call(
        finish_kernel,
        out_shape=(
            jax.ShapeDtypeStruct((slots, 2 * HEAD_DIM), jnp.bfloat16),
            jax.ShapeDtypeStruct((copies, slots, 2 * HEAD_DIM), jnp.bfloat16),
        ),
        name="heavy_finish",
    )(own, arrived)


def out_weights_kernel(pos, mine_ref, theirs_ref, out_ref, *, depth):
    core = pos[2]
    z_size = mine_ref.shape[0]
    for i in range(8):
        for z in range(z_size):
            base = (i * z_size + z) * 2
            out_ref[pl.ds(pl.multiple_of((base + core) * depth, depth), depth), :] = mine_ref[
                z, i * depth : (i + 1) * depth, :
            ]
            out_ref[pl.ds(pl.multiple_of((base + 1 - core) * depth, depth), depth), :] = theirs_ref[
                z, i * depth : (i + 1) * depth, :
            ]


def out_weights(pos, mine, theirs, depth):
    z_size = mine.shape[0]
    shape = (16 * z_size * depth, 2 * HEAD_DIM)
    block = (z_size, mine.shape[1], 2 * HEAD_DIM)
    return pl.pallas_call(
        functools.partial(out_weights_kernel, depth=depth),
        out_shape=jax.ShapeDtypeStruct(shape, jnp.bfloat16),
        grid_spec=pltpu.PrefetchScalarGridSpec(
            num_scalar_prefetch=1,
            grid=(1,),
            in_specs=[spec(block, lambda i, p: (0, 0, 0))] * 2,
            out_specs=spec(shape, lambda i, p: (0, 0)),
        ),
        name="out_weights",
    )(pos, mine, theirs)


def heavy_kernel(q_ref, own_ref, other_ref, bias_ref, w_ref, out_ref):
    keys = own_ref.shape[0]
    q = q_ref[...]
    lane = lax.broadcasted_iota(jnp.int32, (1, 2 * HEAD_DIM), 1)
    scale = HEAD_DIM ** -0.5
    s0 = lax.dot_general(q, own_ref[...], NT, preferred_element_type=jnp.float32) * scale + bias_ref[:, :keys]
    s1 = lax.dot_general(q, other_ref[...], NT, preferred_element_type=jnp.float32) * scale + bias_ref[:, keys:]
    peak = jnp.maximum(jnp.max(s0, axis=1, keepdims=True), jnp.max(s1, axis=1, keepdims=True))
    p0 = jnp.exp(s0 - peak)
    p1 = jnp.exp(s1 - peak)
    total = jnp.sum(p0, axis=1, keepdims=True) + jnp.sum(p1, axis=1, keepdims=True)
    blended = jnp.dot(p0.astype(jnp.bfloat16), own_ref[...], preferred_element_type=jnp.float32)
    blended = blended + jnp.dot(p1.astype(jnp.bfloat16), other_ref[...], preferred_element_type=jnp.float32)
    context = jnp.where(lane >= HEAD_DIM, blended / total, 0.0).astype(jnp.bfloat16)
    part = lax.dot_general(context, w_ref[...], NT, preferred_element_type=jnp.float32).astype(jnp.bfloat16)
    count, capacity, half = out_ref.shape
    for i in range(count):
        top = i // 2 * capacity
        out_ref[i] = part[top : top + capacity, i % 2 * half : (i % 2 + 1) * half]


def heavy_attention(q, own, other, bias, w, group):
    return pl.pallas_call(
        heavy_kernel,
        out_shape=jax.ShapeDtypeStruct((2 * group, q.shape[0] // group, w.shape[0] // 2), jnp.bfloat16),
        name="heavy_attention",
    )(q, own, other, bias, w)


def combine_kernel(own_ref, recv_ref, parts_ref, logit_ref, live_ref, slots_ref, out_ref, hi_ref, lo_ref):
    step = pl.program_id(0)
    block = own_ref.shape[0]

    @pl.when(step == 0)
    def _():
        total = parts_ref[0].astype(jnp.float32)
        for i in range(1, parts_ref.shape[0]):
            total = total + parts_ref[i].astype(jnp.float32)
        gate = jnp.where(live_ref[...] > 0, 1.0 / (1.0 + jnp.exp(-logit_ref[...])), 0.0)
        total = total * gate[:, 0:1]
        hi = total.astype(jnp.bfloat16)
        hi_ref[...] = hi
        lo_ref[...] = (total - hi.astype(jnp.float32)).astype(jnp.bfloat16)

    capacity = slots_ref.shape[1]
    token = lax.broadcasted_iota(jnp.int32, (block, capacity), 0) + step * block
    pick = jnp.where(token == slots_ref[...], 1.0, 0.0).astype(jnp.bfloat16)
    heavy = jnp.dot(pick, hi_ref[...], preferred_element_type=jnp.float32)
    heavy = heavy + jnp.dot(pick, lo_ref[...], preferred_element_type=jnp.float32)
    out_ref[...] = (own_ref[...] + recv_ref[...].astype(jnp.float32) + heavy).astype(jnp.bfloat16)


def combine(own, recv, parts, logit, live, slots):
    rows, cols = own.shape
    capacity = slots.shape[1]
    block = 128
    return pl.pallas_call(
        combine_kernel,
        out_shape=jax.ShapeDtypeStruct((rows, cols), jnp.bfloat16),
        grid=(rows // block,),
        in_specs=[
            spec((block, cols), lambda b: (b, 0)),
            spec((block, cols), lambda b: (b, 0)),
            spec(parts.shape, lambda b: (0, 0, 0)),
            spec((capacity, 128), lambda b: (0, 0)),
            spec((capacity, 128), lambda b: (0, 0)),
            spec((1, capacity), lambda b: (0, 0)),
        ],
        out_specs=spec((block, cols), lambda b: (b, 0)),
        scratch_shapes=[
            pltpu.VMEM((capacity, cols), jnp.bfloat16),
            pltpu.VMEM((capacity, cols), jnp.bfloat16),
        ],
        name="combine",
    )(own, recv, parts, logit, live, slots)


def swap(a, axis):
    return lax.ppermute(a, axis, [(0, 1), (1, 0)])


def layer(
    normed,
    router,
    light_qkv,
    light_out,
    heavy_qkv,
    heavy_out,
    query_slots,
    query_count,
    key_slots,
    key_count,
):
    rows, half = normed.shape
    side = lax.axis_index("xh")
    core = lax.axis_index("c")
    shard_index = lax.axis_index(SEQ)
    shard_total = lax.axis_size(SEQ)
    y_size, _, z_size, _ = (lax.axis_size(axis) for axis in SEQ)
    capacity = query_slots.shape[1]
    feature_rows = heavy_qkv.shape[1]
    heads = heavy_qkv.shape[2] // HEAD_DIM
    group = heads
    pos = jnp.stack([shard_index, side, core, lax.axis_index("y"), lax.axis_index("xl")]).astype(jnp.int32)

    slots = jnp.concatenate([query_slots[0], key_slots[0]])
    pick = (slots[:, None] == jnp.arange(rows, dtype=jnp.int32)[None, :]).astype(jnp.bfloat16)
    routed = jnp.dot(pick, normed, preferred_element_type=jnp.float32).astype(jnp.bfloat16)
    partner = swap(routed, "xl")
    pair = jnp.stack([routed, partner])
    pieces = [pair]
    for d in range(1, y_size):
        pieces.append(lax.ppermute(pair, "y", [(i, (i + d) % y_size) for i in range(y_size)]))

    by_head = pack_heads(key_count, heavy_qkv, heavy_out)
    sliced = lax.all_to_all(by_head, GROUP + ("xh",), 0, 0)
    packed = pack_copies(pos, sliced, z_size)
    mine = lax.all_to_all(packed, "z", 0, 0)
    theirs = swap(mine, "c")
    out_all = out_weights(pos, mine, theirs, feature_rows)

    tail = group * feature_rows
    all_counts = jnp.stack([mine[:, tail:, 0], theirs[:, tail:, 0]], axis=0)
    slot_range = jnp.arange(capacity, dtype=jnp.int32)
    live = slot_range[None, None, None, :] < all_counts.astype(jnp.int32)[..., None]
    bias = jnp.where(live, 0.0, NEG).astype(jnp.float32).reshape(1, shard_total * capacity)

    part_own, part_other = heavy_project(pos, mine, theirs, pieces, feature_rows)
    arrived = swap(part_other, "xh")
    query, copies = finish(part_own, arrived, z_size)
    keys_own = lax.all_to_all(copies, "z", 0, 0)
    keys_other = swap(keys_own, "c")
    keys_own = keys_own.reshape(-1, 2 * HEAD_DIM)
    keys_other = keys_other.reshape(-1, 2 * HEAD_DIM)
    outputs = heavy_attention(query, keys_own, keys_other, bias, out_all, group)
    parts = lax.all_to_all(outputs, GROUP + ("xh",), 0, 0)

    features = swap(normed, "xh")
    partial = project_own(pos, normed, light_qkv)
    paired = project_add(pos, features, light_qkv, partial, 1, 2)
    ends = shard_total - 1
    left = lax.ppermute(paired[:, rows - RADIUS :], SEQ, [(i, i + 1) for i in range(ends)])
    right = lax.ppermute(paired[:, :RADIUS], SEQ, [(i + 1, i) for i in range(ends)])
    queries = project_add(pos, features, light_qkv, partial, 0, 1)
    own, other = light_attention(pos, queries, paired, left, right, light_out, rows * shard_total)
    recv = swap(other, "xh")

    picked = jnp.dot(pick[:capacity], features, preferred_element_type=jnp.float32)
    router_own = lax.dynamic_slice_in_dim(router, side * half, half, 0).astype(jnp.float32)
    router_other = lax.dynamic_slice_in_dim(router, (1 - side) * half, half, 0).astype(jnp.float32)
    logit = jnp.sum(routed[:capacity].astype(jnp.float32) * router_own[None], axis=1)
    logit = logit + jnp.sum(picked * router_other[None], axis=1)
    logit = jnp.broadcast_to(logit[:, None], (capacity, 128))
    query_live = jnp.broadcast_to((slot_range < query_count[0]).astype(jnp.float32)[:, None], (capacity, 128))
    return combine(own, recv, parts, logit, query_live, query_slots)


def solution(mesh):
    fine = Mesh(mesh.devices.reshape(4, 2, 8, 2, 2), SEQ + ("xh",))
    in_specs = (
        P(SEQ, "xh"),
        P(),
        P(None, None, "xh"),
        P("xh", None),
        P(None, SEQ, "xh"),
        P("xh", SEQ),
        P(SEQ, None),
        P(SEQ),
        P(SEQ, None),
        P(SEQ),
    )
    return jax.shard_map(layer, mesh=fine, in_specs=in_specs, out_specs=P(SEQ, "xh"), check_vma=False)
```

```python
import functools

import jax
import jax.numpy as jnp
from jax import lax
from jax.experimental import pallas as pl
from jax.experimental.pallas import tpu as pltpu
from jax.sharding import Mesh
from jax.sharding import PartitionSpec as P

HEAD_DIM = 64
RADIUS = 64
NEG = -1e30
SEQ = ("y", "xl", "z", "c")
GROUP = ("y", "xl")


NT = (((1,), (1,)), ((), ()))


def spec(shape, index):
    return pl.BlockSpec(shape, index)


SMALL = pltpu.CompilerParams(vmem_limit_bytes=20 << 20)
HELD = pl.BlockSpec(memory_space=pltpu.VMEM)


def far(a):
    return pltpu.with_memory_space_constraint(a, pltpu.HBM)


def held(a):
    return pltpu.with_memory_space_constraint(a, pltpu.VMEM)


def project_own_kernel(pos, x_ref, w_ref, out_ref):
    out_ref[pl.program_id(0)] = jnp.dot(x_ref[...], w_ref[0], preferred_element_type=jnp.float32)


def project_own(pos, x, w):
    rows, half = x.shape
    cols = w.shape[2]
    return pl.pallas_call(
        project_own_kernel,
        out_shape=pltpu.VMEM((2, rows, cols), jnp.float32),
        grid_spec=pltpu.PrefetchScalarGridSpec(
            num_scalar_prefetch=1,
            grid=(2,),
            in_specs=[
                spec((rows, half), lambda j, p: (0, 0)),
                spec((1, half, cols), lambda j, p: (j + 1, p[1], 0)),
            ],
            out_specs=HELD,
        ),
        compiler_params=SMALL,
        name="light_project_own",
    )(pos, far(x), far(w))


def project_keys_kernel(pos, x_ref, w_ref, part_ref, out_ref, head_ref, tail_ref):
    j = pl.program_id(0)
    rows = out_ref.shape[1]
    total = jnp.dot(x_ref[...], w_ref[0], preferred_element_type=jnp.float32) + part_ref[j]
    total = total.astype(jnp.bfloat16)
    out_ref[j] = total
    head_ref[j] = total[:RADIUS]
    tail_ref[j] = total[rows - RADIUS :]


def project_keys(pos, x, w, part):
    rows, half = x.shape
    cols = w.shape[2]
    return pl.pallas_call(
        project_keys_kernel,
        out_shape=(
            pltpu.VMEM((2, rows, cols), jnp.bfloat16),
            pltpu.VMEM((2, RADIUS, cols), jnp.bfloat16),
            pltpu.VMEM((2, RADIUS, cols), jnp.bfloat16),
        ),
        grid_spec=pltpu.PrefetchScalarGridSpec(
            num_scalar_prefetch=1,
            grid=(2,),
            in_specs=[HELD, spec((1, half, cols), lambda j, p: (j + 1, 1 - p[1], 0)), HELD],
            out_specs=(HELD, HELD, HELD),
        ),
        compiler_params=SMALL,
        name="light_project_keys",
    )(pos, held(x), far(w), held(part))


def project_queries_kernel(pos, own_ref, other_ref, w_ref, out_ref, part_ref):
    step = pl.program_id(0)

    @pl.when(step == 0)
    def _():
        part_ref[...] = jnp.dot(other_ref[...], w_ref[0], preferred_element_type=jnp.float32)

    @pl.when(step == 1)
    def _():
        total = part_ref[...] + jnp.dot(own_ref[...], w_ref[0], preferred_element_type=jnp.float32)
        out_ref[...] = total.astype(jnp.bfloat16)


def project_queries(pos, own, other, w):
    rows, half = own.shape
    cols = w.shape[2]
    return pl.pallas_call(
        project_queries_kernel,
        out_shape=pltpu.VMEM((rows, cols), jnp.bfloat16),
        grid_spec=pltpu.PrefetchScalarGridSpec(
            num_scalar_prefetch=1,
            grid=(2,),
            in_specs=[
                spec((rows, half), lambda k, p: (0, 0)),
                HELD,
                spec((1, half, cols), lambda k, p: (0, jnp.where(k == 0, 1 - p[1], p[1]), 0)),
            ],
            out_specs=HELD,
            scratch_shapes=[pltpu.VMEM((rows, cols), jnp.float32)],
        ),
        compiler_params=SMALL,
        name="light_project_queries",
    )(pos, far(own), held(other), far(w))


def light_block(pos, block, q_ref, kv_ref, left, right, tokens):
    size = 128
    length = kv_ref.shape[1]
    width = q_ref.shape[1]
    span = size + 2 * RADIUS
    low, high = block * size - RADIUS, (block + 1) * size + RADIUS
    row = lax.broadcasted_iota(jnp.int32, (size, span), 0)
    col = lax.broadcasted_iota(jnp.int32, (size, span), 1)
    key = pos[0] * length + low + col
    allowed = (col >= row) & (col - row <= 2 * RADIUS) & (key >= 0) & (key < tokens)
    bias = jnp.where(allowed, 0.0, NEG)
    bias = jnp.concatenate([bias, bias], axis=0)
    lane = lax.broadcasted_iota(jnp.int32, (size, 2 * HEAD_DIM), 1)
    first = lane < HEAD_DIM

    def window(which, lanes):
        pieces = []
        if low < 0:
            pieces.append(left[which, :, lanes])
        pieces.append(kv_ref[which, max(low, 0) : min(high, length), lanes])
        if high > length:
            pieces.append(right[which, :, lanes])
        return pieces[0] if len(pieces) == 1 else jnp.concatenate(pieces, axis=0)

    pieces = []
    for pair in range(width // (2 * HEAD_DIM)):
        lanes = slice(pair * 2 * HEAD_DIM, (pair + 1) * 2 * HEAD_DIM)
        q = q_ref[block * size : (block + 1) * size, lanes]
        k = window(0, lanes)
        v = window(1, lanes)
        zero = jnp.zeros_like(q)
        both = jnp.concatenate([jnp.where(first, q, zero), jnp.where(first, zero, q)], axis=0)
        scores = lax.dot_general(both, k, NT, preferred_element_type=jnp.float32)
        scores = scores * (HEAD_DIM ** -0.5) + bias
        peak = jnp.max(scores, axis=1, keepdims=True)
        weights = jnp.exp(scores - peak)
        total = jnp.sum(weights, axis=1, keepdims=True)
        blended = jnp.dot(weights.astype(jnp.bfloat16), v, preferred_element_type=jnp.float32) / total
        pieces.append(jnp.where(first, blended[:size], blended[size:]).astype(jnp.bfloat16))
    return jnp.concatenate(pieces, axis=1)


def light_kernel(pos, q_ref, kv_ref, left, right, out_ref, *, tokens):
    size = 128
    for block in (1, 2, 0, 3):
        out_ref[block * size : (block + 1) * size, :] = light_block(pos, block, q_ref, kv_ref, left, right, tokens)


def light_attention(pos, q, kv, left, right, tokens):
    return pl.pallas_call(
        functools.partial(light_kernel, tokens=tokens),
        out_shape=pltpu.VMEM(q.shape, jnp.bfloat16),
        grid_spec=pltpu.PrefetchScalarGridSpec(
            num_scalar_prefetch=1,
            grid=(1,),
            in_specs=[HELD] * 4,
            out_specs=HELD,
        ),
        compiler_params=SMALL,
        name="light_attention",
    )(pos, *[held(a) for a in (q, kv, left, right)])


def light_product_kernel(pos, own_ref, recv_ref, own_w_ref, mine_w_ref, theirs_w_ref, out_ref):
    core = pos[2]
    depth = mine_w_ref.shape[0]
    first = recv_ref[:, pl.ds(pl.multiple_of(core * depth, depth), depth)]
    second = recv_ref[:, pl.ds(pl.multiple_of((1 - core) * depth, depth), depth)]
    total = jnp.dot(own_ref[...], own_w_ref[...], preferred_element_type=jnp.float32)
    total = total + jnp.dot(first, mine_w_ref[...], preferred_element_type=jnp.float32)
    out_ref[...] = total + jnp.dot(second, theirs_w_ref[...], preferred_element_type=jnp.float32)


def light_product(pos, own, recv, own_w, mine_w, theirs_w):
    rows, width = own.shape
    half, depth = mine_w.shape[1], mine_w.shape[0]
    block = half // 2
    whole = lambda j, p: (0, 0)
    column = lambda j, p: (0, j)
    return pl.pallas_call(
        light_product_kernel,
        out_shape=jax.ShapeDtypeStruct((rows, half), jnp.float32),
        grid_spec=pltpu.PrefetchScalarGridSpec(
            num_scalar_prefetch=1,
            grid=(2,),
            in_specs=[
                spec((rows, width), whole),
                spec((rows, width), whole),
                spec((width, block), lambda j, p: (0, 2 * p[1] + j)),
                spec((depth, block), column),
                spec((depth, block), column),
            ],
            out_specs=spec((rows, block), column),
        ),
        compiler_params=SMALL,
        name="light_product",
    )(pos, own, recv, far(own_w), mine_w, theirs_w)


def pack_heads_kernel(counts, qkv_ref, out_w_ref, packed_ref):
    depth = qkv_ref.shape[1]
    heads = qkv_ref.shape[2] // HEAD_DIM
    turned = out_w_ref[...]
    shape = (packed_ref.shape[1] - depth, packed_ref.shape[2])
    marks = jnp.where(lax.broadcasted_iota(jnp.int32, shape, 1) < 2 * HEAD_DIM, counts[0], counts[1])
    marks = marks.astype(jnp.float32).astype(jnp.bfloat16)
    for h in range(heads):
        lanes = slice(h * HEAD_DIM, (h + 1) * HEAD_DIM)
        piece = jnp.concatenate([qkv_ref[0, :, lanes], turned[:, lanes], qkv_ref[1, :, lanes], qkv_ref[2, :, lanes]], axis=1)
        for side in range(2):
            packed_ref[2 * h + side, 0:depth, :] = piece
            packed_ref[2 * h + side, depth:, :] = marks


def pack_heads(count, qkv, out_w):
    depth = qkv.shape[1]
    heads = qkv.shape[2] // HEAD_DIM
    return pl.pallas_call(
        pack_heads_kernel,
        out_shape=jax.ShapeDtypeStruct((2 * heads, depth + 8, 4 * HEAD_DIM), jnp.bfloat16),
        grid_spec=pltpu.PrefetchScalarGridSpec(
            num_scalar_prefetch=1,
            grid=(1,),
            in_specs=[spec(qkv.shape, lambda i, p: (0, 0, 0)), spec(out_w.shape, lambda i, p: (0, 0))],
            out_specs=spec((2 * heads, depth + 8, 4 * HEAD_DIM), lambda i, p: (0, 0, 0)),
        ),
        compiler_params=SMALL,
        name="pack_heads",
    )(count, far(qkv), far(out_w))


def pack_copies_kernel(pos, in_ref, out_ref, *, depth):
    side = pos[1]
    copies = out_ref.shape[0]
    group = in_ref.shape[0] // 2
    lane = lax.broadcasted_iota(jnp.int32, (depth, 4 * HEAD_DIM), 1)
    from_out = (lane >= HEAD_DIM) & (lane < 2 * HEAD_DIM)
    marks = []
    for i in range(group):
        qkv = in_ref[side * group + i, 0:depth, :]
        out_w = in_ref[2 * i + side, 0:depth, :]
        tile = jnp.where(from_out, out_w, qkv)
        marks.append(in_ref[2 * i + side, depth : depth + 1, :])
        for t in range(copies):
            out_ref[t, i * depth : (i + 1) * depth, :] = tile
    marks = jnp.concatenate(marks, axis=0)
    for t in range(copies):
        out_ref[t, group * depth :, :] = marks


def pack_copies(pos, sliced, copies):
    group = sliced.shape[0] // 2
    depth = sliced.shape[1] - 8
    shape = (copies, group * depth + group, 4 * HEAD_DIM)
    return pl.pallas_call(
        functools.partial(pack_copies_kernel, depth=depth),
        out_shape=jax.ShapeDtypeStruct(shape, jnp.bfloat16),
        grid_spec=pltpu.PrefetchScalarGridSpec(
            num_scalar_prefetch=1,
            grid=(1,),
            in_specs=[HELD],
            out_specs=spec(shape, lambda i, p: (0, 0, 0)),
        ),
        compiler_params=SMALL,
        name="pack_copies",
    )(pos, held(sliced))


def heavy_project_kernel(
    pos, mine_ref, theirs_ref, r0, r1, r2, r3, router_ref, own_ref, other_ref, w_ref, *, depth, capacity
):
    side, core, y, xl = pos[1], pos[2], pos[3], pos[4]
    z_size = mine_ref.shape[0]
    for y_half in range(2):
        for x in range(2):
            for m in range(2):
                i = (y_half * 2 + x) * 2 + m
                for z in range(z_size):
                    base = ((y_half * 2 + x) * z_size + z) * 2
                    w_ref[m, pl.ds(pl.multiple_of((base + core) * depth, depth), depth), :] = mine_ref[
                        z, i * depth : (i + 1) * depth, :
                    ]
                    w_ref[m, pl.ds(pl.multiple_of((base + 1 - core) * depth, depth), depth), :] = theirs_ref[
                        z, i * depth : (i + 1) * depth, :
                    ]
    lane = lax.broadcasted_iota(jnp.int32, (capacity, 2 * HEAD_DIM), 1)
    keep = lane < HEAD_DIM
    upper = lane < HEAD_DIM + HEAD_DIM // 2
    own_w = w_ref[side]
    other_w = w_ref[1 - side]
    for d, piece in enumerate((r0, r1, r2, r3)):
        rows = piece[...].reshape(4 * capacity, piece.shape[2])
        for_other = jnp.dot(rows, other_w, preferred_element_type=jnp.float32)
        for_own = jnp.dot(rows, own_w, preferred_element_type=jnp.float32)
        score = jnp.dot(rows, router_ref[...], preferred_element_type=jnp.float32)
        high = score.astype(jnp.bfloat16).astype(jnp.float32)
        source_y = lax.rem(y - d + 4, 4)
        for which in range(2):
            source = source_y * 2 + (xl if which == 0 else 1 - xl)
            query = slice(which * 2 * capacity, which * 2 * capacity + capacity)
            keys = slice(query.stop, query.stop + capacity)
            at = pl.ds(pl.multiple_of(source * capacity, capacity), capacity)
            terms = jnp.where(upper, high[query], score[query] - high[query])
            left = jnp.where(keep, for_other[query, : 2 * HEAD_DIM], terms)
            other_ref[at, :] = jnp.concatenate([left, for_other[keys, 2 * HEAD_DIM :]], axis=1).astype(jnp.bfloat16)
            left = jnp.where(keep, for_own[query, : 2 * HEAD_DIM], score[query])
            own_ref[at, :] = jnp.concatenate([left, for_own[keys, 2 * HEAD_DIM :]], axis=1)


def heavy_project(pos, mine, theirs, pieces, router, depth):
    capacity = pieces[0].shape[1] // 2
    half = pieces[0].shape[2]
    slots = 8 * capacity
    return pl.pallas_call(
        functools.partial(heavy_project_kernel, depth=depth, capacity=capacity),
        out_shape=(
            pltpu.VMEM((slots, 4 * HEAD_DIM), jnp.float32),
            pltpu.VMEM((slots, 4 * HEAD_DIM), jnp.bfloat16),
        ),
        grid_spec=pltpu.PrefetchScalarGridSpec(
            num_scalar_prefetch=1,
            grid=(1,),
            in_specs=[HELD] * (3 + len(pieces)),
            out_specs=(HELD, HELD),
            scratch_shapes=[pltpu.VMEM((2, half, 4 * HEAD_DIM), jnp.bfloat16)],
        ),
        compiler_params=SMALL,
        name="heavy_project",
    )(pos, held(mine), held(theirs), *[held(p) for p in pieces], held(router))


def finish_kernel(pos, own_ref, arrived_ref, mine_ref, query_ref, gate_ref, copies_ref, *, capacity):
    own = own_ref[...]
    arrived = arrived_ref[...].astype(jnp.float32)
    total = (own + arrived).astype(jnp.bfloat16)
    lane = lax.broadcasted_iota(jnp.int32, (own.shape[0], 2 * HEAD_DIM), 1)
    query_ref[...] = jnp.where(lane < HEAD_DIM, total[:, : 2 * HEAD_DIM].astype(jnp.float32), 0.0).astype(jnp.bfloat16)
    for t in range(copies_ref.shape[0]):
        copies_ref[t] = total[:, 2 * HEAD_DIM :]
    middle = HEAD_DIM + HEAD_DIM // 2
    logit = own[:, HEAD_DIM : HEAD_DIM + 1] + arrived[:, HEAD_DIM : HEAD_DIM + 1] + arrived[:, middle : middle + 1]
    gate = jnp.broadcast_to(1.0 / (1.0 + jnp.exp(-logit)), gate_ref.shape)
    group = own.shape[0] // capacity
    tail = mine_ref.shape[1] - group
    marks = mine_ref[pos[5], tail:, 2 * HEAD_DIM :].astype(jnp.float32)
    slot = lax.broadcasted_iota(jnp.int32, (capacity, 2 * HEAD_DIM), 0).astype(jnp.float32)
    for g in range(group):
        rows = slice(g * capacity, (g + 1) * capacity)
        gate_ref[rows, :] = jnp.where(slot < marks[g : g + 1, :], gate[rows], 0.0)


def finish(pos, own, arrived, mine, capacity):
    slots = own.shape[0]
    copies = mine.shape[0]
    return pl.pallas_call(
        functools.partial(finish_kernel, capacity=capacity),
        out_shape=(
            pltpu.VMEM((slots, 2 * HEAD_DIM), jnp.bfloat16),
            pltpu.VMEM((slots, 2 * HEAD_DIM), jnp.float32),
            pltpu.HBM((copies, slots, 2 * HEAD_DIM), jnp.bfloat16),
        ),
        grid_spec=pltpu.PrefetchScalarGridSpec(
            num_scalar_prefetch=1,
            grid=(1,),
            in_specs=[HELD, HELD, HELD],
            out_specs=(HELD, HELD, spec((copies, slots, 2 * HEAD_DIM), lambda i, p: (0, 0, 0))),
        ),
        compiler_params=SMALL,
        name="heavy_finish",
    )(pos, held(own), held(arrived), held(mine))


def out_weights_kernel(pos, mine_ref, theirs_ref, out_ref, bias_ref, *, depth, capacity):
    core = pos[2]
    z_size = mine_ref.shape[0]
    group = 8
    for i in range(group):
        for z in range(z_size):
            base = (i * z_size + z) * 2
            tile = slice(i * depth, (i + 1) * depth)
            out_ref[pl.ds(pl.multiple_of((base + core) * depth, depth), depth), :] = mine_ref[z, tile, : 2 * HEAD_DIM]
            out_ref[pl.ds(pl.multiple_of((base + 1 - core) * depth, depth), depth), :] = theirs_ref[
                z, tile, : 2 * HEAD_DIM
            ]
    lane = lax.broadcasted_iota(jnp.int32, (1, 2 * HEAD_DIM), 1)
    per_row = 2 * HEAD_DIM // capacity
    for which, ref in enumerate((mine_ref, theirs_ref)):
        for z in range(z_size):
            marks = ref[z, group * depth : group * depth + group, : 2 * HEAD_DIM].astype(jnp.float32)
            for part in range(group // per_row):
                count = jnp.zeros((1, 2 * HEAD_DIM), jnp.float32)
                for j in range(per_row):
                    g = part * per_row + j
                    count = jnp.where(lane // capacity == j, marks[g : g + 1, :], count)
                live = (lane % capacity).astype(jnp.float32) < count
                at = ((which * z_size + z) * (group // per_row) + part) * 2 * HEAD_DIM
                bias_ref[:, at : at + 2 * HEAD_DIM] = jnp.where(live, 0.0, NEG)


def out_weights(pos, mine, theirs, depth, capacity):
    z_size = mine.shape[0]
    return pl.pallas_call(
        functools.partial(out_weights_kernel, depth=depth, capacity=capacity),
        out_shape=(
            pltpu.VMEM((16 * z_size * depth, 2 * HEAD_DIM), jnp.bfloat16),
            pltpu.VMEM((1, 16 * z_size * capacity), jnp.float32),
        ),
        grid_spec=pltpu.PrefetchScalarGridSpec(
            num_scalar_prefetch=1,
            grid=(1,),
            in_specs=[HELD, HELD],
            out_specs=(HELD, HELD),
        ),
        compiler_params=SMALL,
        name="out_weights",
    )(pos, held(mine), held(theirs))


def heavy_kernel(q_ref, own_ref, other_ref, bias_ref, w_ref, gate_ref, out_ref):
    keys = own_ref.shape[0]
    q = q_ref[...]
    lane = lax.broadcasted_iota(jnp.int32, (1, 2 * HEAD_DIM), 1)
    scale = HEAD_DIM ** -0.5
    s0 = lax.dot_general(q, own_ref[...], NT, preferred_element_type=jnp.float32) * scale + bias_ref[:, :keys]
    s1 = lax.dot_general(q, other_ref[...], NT, preferred_element_type=jnp.float32) * scale + bias_ref[:, keys:]
    peak = jnp.maximum(jnp.max(s0, axis=1, keepdims=True), jnp.max(s1, axis=1, keepdims=True))
    p0 = jnp.exp(s0 - peak)
    p1 = jnp.exp(s1 - peak)
    total = jnp.sum(p0, axis=1, keepdims=True) + jnp.sum(p1, axis=1, keepdims=True)
    blended = jnp.dot(p0.astype(jnp.bfloat16), own_ref[...], preferred_element_type=jnp.float32)
    blended = blended + jnp.dot(p1.astype(jnp.bfloat16), other_ref[...], preferred_element_type=jnp.float32)
    context = jnp.where(lane >= HEAD_DIM, blended / total, 0.0).astype(jnp.bfloat16)
    part = lax.dot_general(context, w_ref[...], NT, preferred_element_type=jnp.float32)
    part = (part * gate_ref[:, 0:1]).astype(jnp.bfloat16)
    count, capacity, half = out_ref.shape
    for i in range(count):
        top = i // 2 * capacity
        out_ref[i] = part[top : top + capacity, i % 2 * half : (i % 2 + 1) * half]


def heavy_attention(q, own, other, bias, w, gate, group):
    return pl.pallas_call(
        heavy_kernel,
        out_shape=jax.ShapeDtypeStruct((2 * group, q.shape[0] // group, w.shape[0] // 2), jnp.bfloat16),
        in_specs=[HELD] * 6,
        compiler_params=SMALL,
        name="heavy_attention",
    )(*[held(a) for a in (q, own, other, bias, w, gate)])


def combine_kernel(own_ref, parts_ref, slots_ref, out_ref, hi_ref, lo_ref):
    step = pl.program_id(0)
    block = out_ref.shape[0]

    @pl.when(step == 0)
    def _():
        total = parts_ref[0].astype(jnp.float32)
        for i in range(1, parts_ref.shape[0]):
            total = total + parts_ref[i].astype(jnp.float32)
        hi = total.astype(jnp.bfloat16)
        hi_ref[...] = hi
        lo_ref[...] = (total - hi.astype(jnp.float32)).astype(jnp.bfloat16)

    capacity = slots_ref.shape[1]
    token = lax.broadcasted_iota(jnp.int32, (block, capacity), 0) + step * block
    pick = jnp.where(token == slots_ref[...], 1.0, 0.0).astype(jnp.bfloat16)
    heavy = jnp.dot(pick, hi_ref[...], preferred_element_type=jnp.float32)
    heavy = heavy + jnp.dot(pick, lo_ref[...], preferred_element_type=jnp.float32)
    out_ref[...] = (own_ref[...] + heavy).astype(jnp.bfloat16)


def combine(own, parts, slots):
    rows, cols = own.shape
    capacity = slots.shape[1]
    block = 128
    return pl.pallas_call(
        combine_kernel,
        out_shape=jax.ShapeDtypeStruct((rows, cols), jnp.bfloat16),
        grid=(rows // block,),
        in_specs=[spec((block, cols), lambda b: (b, 0)), HELD, spec((1, capacity), lambda b: (0, 0))],
        out_specs=spec((block, cols), lambda b: (b, 0)),
        scratch_shapes=[
            pltpu.VMEM((capacity, cols), jnp.bfloat16),
            pltpu.VMEM((capacity, cols), jnp.bfloat16),
        ],
        compiler_params=SMALL,
        name="combine",
    )(own, held(parts), slots)


def swap(a, axis):
    return lax.ppermute(a, axis, [(0, 1), (1, 0)])


def layer(
    normed,
    router,
    light_qkv,
    light_out,
    heavy_qkv,
    heavy_out,
    query_slots,
    query_count,
    key_slots,
    key_count,
):
    rows, half = normed.shape
    side = lax.axis_index("xh")
    core = lax.axis_index("c")
    shard_index = lax.axis_index(SEQ)
    shard_total = lax.axis_size(SEQ)
    y_size, _, z_size, _ = (lax.axis_size(axis) for axis in SEQ)
    capacity = query_slots.shape[1]
    feature_rows = heavy_qkv.shape[1]
    heads = heavy_qkv.shape[2] // HEAD_DIM
    group = heads
    pos = jnp.stack([shard_index, side, core, lax.axis_index("y"), lax.axis_index("xl"), lax.axis_index("z")]).astype(jnp.int32)

    slots = jnp.concatenate([query_slots[0], key_slots[0]])
    pick = (slots[:, None] == jnp.arange(rows, dtype=jnp.int32)[None, :]).astype(jnp.bfloat16)
    routed = jnp.dot(pick, normed, preferred_element_type=jnp.float32).astype(jnp.bfloat16)
    partner = swap(routed, "xl")
    pair = jnp.stack([routed, partner])
    router_own = lax.dynamic_slice_in_dim(router, side * half, half, 0)
    router_own = jnp.broadcast_to(router_own[:, None], (half, 2 * HEAD_DIM))
    pieces = [pair]
    for d in range(1, y_size):
        pieces.append(lax.ppermute(pair, "y", [(i, (i + d) % y_size) for i in range(y_size)]))

    by_head = pack_heads(jnp.concatenate([key_count, query_count]), heavy_qkv, jnp.transpose(heavy_out))
    sliced = lax.all_to_all(by_head, GROUP + ("xh",), 0, 0)
    packed = pack_copies(pos, sliced, z_size)
    mine = lax.all_to_all(packed, "z", 0, 0)
    theirs = swap(mine, "c")
    out_all, bias = out_weights(pos, mine, theirs, feature_rows, capacity)

    part_own, part_other = heavy_project(pos, mine, theirs, pieces, router_own, feature_rows)
    arrived = swap(part_other, "xh")
    query, gate, copies = finish(pos, part_own, arrived, mine, capacity)
    keys_own = lax.all_to_all(copies, "z", 0, 0)
    keys_other = swap(keys_own, "c")
    keys_own = keys_own.reshape(-1, 2 * HEAD_DIM)
    keys_other = keys_other.reshape(-1, 2 * HEAD_DIM)
    outputs = heavy_attention(query, keys_own, keys_other, bias, out_all, gate, group)
    parts = lax.all_to_all(outputs, GROUP + ("xh",), 0, 0)

    features = swap(normed, "xh")
    partial = project_own(pos, normed, light_qkv)
    paired, head, tail = project_keys(pos, features, light_qkv, partial)
    ends = shard_total - 1
    left = lax.ppermute(tail, SEQ, [(i, i + 1) for i in range(ends)])
    right = lax.ppermute(head, SEQ, [(i + 1, i) for i in range(ends)])
    queries = project_queries(pos, normed, features, light_qkv)
    context = light_attention(pos, queries, paired, left, right, rows * shard_total)
    context_recv = swap(context, "xh")

    depth = light_out.shape[0] // 2
    cut = lax.dynamic_slice(light_out, (core * depth, (1 - side) * half), (depth, half))
    mine_w = lax.ppermute(cut, ("xl", "xh"), [(i, 3 - i) for i in range(4)])
    theirs_w = swap(mine_w, "c")
    own = light_product(pos, context, context_recv, light_out, mine_w, theirs_w)
    return combine(own, parts, query_slots)


def solution(mesh):
    fine = Mesh(mesh.devices.reshape(4, 2, 8, 2, 2), SEQ + ("xh",))
    in_specs = (
        P(SEQ, "xh"),
        P(),
        P(None, None, "xh"),
        P("xh", None),
        P(None, SEQ, "xh"),
        P("xh", SEQ),
        P(SEQ, None),
        P(SEQ),
        P(SEQ, None),
        P(SEQ),
    )
    return jax.shard_map(layer, mesh=fine, in_specs=in_specs, out_specs=P(SEQ, "xh"), check_vma=False)
```

```python
import functools

import jax
import jax.numpy as jnp
from jax import lax
from jax.experimental import pallas as pl
from jax.experimental.pallas import tpu as pltpu
from jax.sharding import Mesh
from jax.sharding import PartitionSpec as P

HEAD_DIM = 64
RADIUS = 64
NEG = -1e30
SEQ = ("y", "xl", "z", "c")
GROUP = ("y", "xl")


NT = (((1,), (1,)), ((), ()))


def spec(shape, index):
    return pl.BlockSpec(shape, index)


SMALL = pltpu.CompilerParams(vmem_limit_bytes=20 << 20)
HELD = pl.BlockSpec(memory_space=pltpu.VMEM)


def far(a):
    return pltpu.with_memory_space_constraint(a, pltpu.HBM)


def held(a):
    return pltpu.with_memory_space_constraint(a, pltpu.VMEM)


def project_own_kernel(pos, x_ref, w_ref, out_ref):
    out_ref[pl.program_id(0)] = jnp.dot(x_ref[...], w_ref[0], preferred_element_type=jnp.float32)


def project_own(pos, x, w):
    rows, half = x.shape
    cols = w.shape[2]
    return pl.pallas_call(
        project_own_kernel,
        out_shape=pltpu.VMEM((2, rows, cols), jnp.float32),
        grid_spec=pltpu.PrefetchScalarGridSpec(
            num_scalar_prefetch=1,
            grid=(2,),
            in_specs=[
                spec((rows, half), lambda j, p: (0, 0)),
                spec((1, half, cols), lambda j, p: (j + 1, p[1], 0)),
            ],
            out_specs=HELD,
        ),
        compiler_params=SMALL,
        name="light_project_own",
    )(pos, far(x), far(w))


def project_keys_kernel(pos, x_ref, w_ref, part_ref, out_ref, inner_ref, outer_ref):
    j = pl.program_id(0)
    rows = out_ref.shape[1]
    total = jnp.dot(x_ref[...], w_ref[0], preferred_element_type=jnp.float32) + part_ref[j]
    total = total.astype(jnp.bfloat16)
    out_ref[0] = total
    head = total[:RADIUS]
    tail = total[rows - RADIUS :]
    even = pos[2] == 0
    inner_ref[j] = jnp.where(even, tail, head)
    outer_ref[j] = jnp.where(even, head, tail)


def project_keys(pos, x, w, part):
    rows, half = x.shape
    cols = w.shape[2]
    return pl.pallas_call(
        project_keys_kernel,
        out_shape=(
            pltpu.HBM((2, rows, cols), jnp.bfloat16),
            pltpu.VMEM((2, RADIUS, cols), jnp.bfloat16),
            pltpu.VMEM((2, RADIUS, cols), jnp.bfloat16),
        ),
        grid_spec=pltpu.PrefetchScalarGridSpec(
            num_scalar_prefetch=1,
            grid=(2,),
            in_specs=[HELD, spec((1, half, cols), lambda j, p: (j + 1, 1 - p[1], 0)), HELD],
            out_specs=(spec((1, rows, cols), lambda j, p: (j, 0, 0)), HELD, HELD),
        ),
        compiler_params=SMALL,
        name="light_project_keys",
    )(pos, held(x), far(w), held(part))


def project_queries_kernel(pos, own_ref, other_ref, w_ref, out_ref, part_ref):
    step = pl.program_id(0)

    @pl.when(step == 0)
    def _():
        part_ref[...] = jnp.dot(other_ref[...], w_ref[0], preferred_element_type=jnp.float32)

    @pl.when(step == 1)
    def _():
        total = part_ref[...] + jnp.dot(own_ref[...], w_ref[0], preferred_element_type=jnp.float32)
        out_ref[...] = total.astype(jnp.bfloat16)


def project_queries(pos, own, other, w):
    rows, half = own.shape
    cols = w.shape[2]
    return pl.pallas_call(
        project_queries_kernel,
        out_shape=pltpu.VMEM((rows, cols), jnp.bfloat16),
        grid_spec=pltpu.PrefetchScalarGridSpec(
            num_scalar_prefetch=1,
            grid=(2,),
            in_specs=[
                spec((rows, half), lambda k, p: (0, 0)),
                HELD,
                spec((1, half, cols), lambda k, p: (0, jnp.where(k == 0, 1 - p[1], p[1]), 0)),
            ],
            out_specs=HELD,
            scratch_shapes=[pltpu.VMEM((rows, cols), jnp.float32)],
        ),
        compiler_params=SMALL,
        name="light_project_queries",
    )(pos, far(own), held(other), far(w))


def light_block(pos, block, q_ref, kv_ref, inner, outer, tokens):
    size = 128
    length = kv_ref.shape[1]
    width = q_ref.shape[1]
    span = size + 2 * RADIUS
    low, high = block * size - RADIUS, (block + 1) * size + RADIUS
    row = lax.broadcasted_iota(jnp.int32, (size, span), 0)
    col = lax.broadcasted_iota(jnp.int32, (size, span), 1)
    key = pos[0] * length + low + col
    allowed = (col >= row) & (col - row <= 2 * RADIUS) & (key >= 0) & (key < tokens)
    bias = jnp.where(allowed, 0.0, NEG)
    bias = jnp.concatenate([bias, bias], axis=0)
    lane = lax.broadcasted_iota(jnp.int32, (size, 2 * HEAD_DIM), 1)
    first = lane < HEAD_DIM

    even = pos[2] == 0

    def window(which, lanes):
        pieces = []
        if low < 0:
            pieces.append(jnp.where(even, outer[which, :, lanes], inner[which, :, lanes]))
        pieces.append(kv_ref[which, max(low, 0) : min(high, length), lanes])
        if high > length:
            pieces.append(jnp.where(even, inner[which, :, lanes], outer[which, :, lanes]))
        return pieces[0] if len(pieces) == 1 else jnp.concatenate(pieces, axis=0)

    pieces = []
    for pair in range(width // (2 * HEAD_DIM)):
        lanes = slice(pair * 2 * HEAD_DIM, (pair + 1) * 2 * HEAD_DIM)
        q = q_ref[block * size : (block + 1) * size, lanes]
        k = window(0, lanes)
        v = window(1, lanes)
        zero = jnp.zeros_like(q)
        both = jnp.concatenate([jnp.where(first, q, zero), jnp.where(first, zero, q)], axis=0)
        scores = lax.dot_general(both, k, NT, preferred_element_type=jnp.float32)
        scores = scores * (HEAD_DIM ** -0.5) + bias
        peak = jnp.max(scores, axis=1, keepdims=True)
        weights = jnp.exp(scores - peak)
        total = jnp.sum(weights, axis=1, keepdims=True)
        blended = jnp.dot(weights.astype(jnp.bfloat16), v, preferred_element_type=jnp.float32) / total
        pieces.append(jnp.where(first, blended[:size], blended[size:]).astype(jnp.bfloat16))
    return jnp.concatenate(pieces, axis=1)


def light_kernel(pos, q_ref, kv_ref, inner, outer, out_ref, *, tokens):
    size = 128
    for block in (1, 2, 0, 3):
        out_ref[block * size : (block + 1) * size, :] = light_block(pos, block, q_ref, kv_ref, inner, outer, tokens)


def light_attention(pos, q, kv, inner, outer, tokens):
    return pl.pallas_call(
        functools.partial(light_kernel, tokens=tokens),
        out_shape=pltpu.VMEM(q.shape, jnp.bfloat16),
        grid_spec=pltpu.PrefetchScalarGridSpec(
            num_scalar_prefetch=1,
            grid=(1,),
            in_specs=[HELD] * 4,
            out_specs=HELD,
        ),
        compiler_params=SMALL,
        name="light_attention",
    )(pos, *[held(a) for a in (q, kv, inner, outer)])


def light_product_kernel(pos, own_ref, recv_ref, own_w_ref, mine_w_ref, theirs_w_ref, out_ref):
    core = pos[2]
    depth = mine_w_ref.shape[0]
    first = recv_ref[:, pl.ds(pl.multiple_of(core * depth, depth), depth)]
    second = recv_ref[:, pl.ds(pl.multiple_of((1 - core) * depth, depth), depth)]
    total = jnp.dot(own_ref[...], own_w_ref[...], preferred_element_type=jnp.float32)
    total = total + jnp.dot(first, mine_w_ref[...], preferred_element_type=jnp.float32)
    out_ref[...] = total + jnp.dot(second, theirs_w_ref[...], preferred_element_type=jnp.float32)


def light_product(pos, own, recv, own_w, mine_w, theirs_w):
    rows, width = own.shape
    half, depth = mine_w.shape[1], mine_w.shape[0]
    block = half // 2
    whole = lambda j, p: (0, 0)
    column = lambda j, p: (0, j)
    return pl.pallas_call(
        light_product_kernel,
        out_shape=jax.ShapeDtypeStruct((rows, half), jnp.float32),
        grid_spec=pltpu.PrefetchScalarGridSpec(
            num_scalar_prefetch=1,
            grid=(2,),
            in_specs=[
                spec((rows, width), whole),
                spec((rows, width), whole),
                spec((width, block), lambda j, p: (0, 2 * p[1] + j)),
                spec((depth, block), column),
                spec((depth, block), column),
            ],
            out_specs=spec((rows, block), column),
        ),
        compiler_params=SMALL,
        name="light_product",
    )(pos, own, recv, far(own_w), mine_w, theirs_w)


def pack_heads_kernel(key_count, query_count, qkv_ref, out_w_ref, packed_ref):
    depth = qkv_ref.shape[1]
    heads = qkv_ref.shape[2] // HEAD_DIM
    turned = out_w_ref[...]
    shape = (packed_ref.shape[1] - depth, packed_ref.shape[2])
    lane = lax.broadcasted_iota(jnp.int32, shape, 1)
    keys = jnp.broadcast_to(key_count[...], shape)
    queries = jnp.broadcast_to(query_count[...], shape)
    marks = jnp.where(lane < 2 * HEAD_DIM, keys, queries).astype(jnp.float32).astype(jnp.bfloat16)
    for h in range(heads):
        lanes = slice(h * HEAD_DIM, (h + 1) * HEAD_DIM)
        piece = jnp.concatenate([qkv_ref[0, :, lanes], turned[:, lanes], qkv_ref[1, :, lanes], qkv_ref[2, :, lanes]], axis=1)
        for side in range(2):
            packed_ref[2 * h + side, 0:depth, :] = piece
            packed_ref[2 * h + side, depth:, :] = marks


def pack_heads(key_count, query_count, qkv, out_w):
    depth = qkv.shape[1]
    heads = qkv.shape[2] // HEAD_DIM
    one = spec((1, 1), lambda i: (0, 0))
    return pl.pallas_call(
        pack_heads_kernel,
        out_shape=jax.ShapeDtypeStruct((2 * heads, depth + 8, 4 * HEAD_DIM), jnp.bfloat16),
        grid=(1,),
        in_specs=[one, one, spec(qkv.shape, lambda i: (0, 0, 0)), spec(out_w.shape, lambda i: (0, 0))],
        out_specs=spec((2 * heads, depth + 8, 4 * HEAD_DIM), lambda i: (0, 0, 0)),
        compiler_params=SMALL,
        name="pack_heads",
    )(key_count.reshape(1, 1), query_count.reshape(1, 1), far(qkv), far(out_w))


def pack_copies_kernel(pos, in_ref, out_ref, *, depth):
    side = pos[1]
    copies = out_ref.shape[0]
    group = in_ref.shape[0] // 2
    lane = lax.broadcasted_iota(jnp.int32, (depth, 4 * HEAD_DIM), 1)
    from_out = (lane >= HEAD_DIM) & (lane < 2 * HEAD_DIM)
    marks = []
    for i in range(group):
        qkv = in_ref[side * group + i, 0:depth, :]
        out_w = in_ref[2 * i + side, 0:depth, :]
        tile = jnp.where(from_out, out_w, qkv)
        marks.append(in_ref[2 * i + side, depth : depth + 1, :])
        for t in range(copies):
            out_ref[t, i * depth : (i + 1) * depth, :] = tile
    marks = jnp.concatenate(marks, axis=0)
    for t in range(copies):
        out_ref[t, group * depth :, :] = marks


def pack_copies(pos, sliced, copies):
    group = sliced.shape[0] // 2
    depth = sliced.shape[1] - 8
    shape = (copies, group * depth + group, 4 * HEAD_DIM)
    return pl.pallas_call(
        functools.partial(pack_copies_kernel, depth=depth),
        out_shape=jax.ShapeDtypeStruct(shape, jnp.bfloat16),
        grid_spec=pltpu.PrefetchScalarGridSpec(
            num_scalar_prefetch=1,
            grid=(1,),
            in_specs=[HELD],
            out_specs=spec(shape, lambda i, p: (0, 0, 0)),
        ),
        compiler_params=SMALL,
        name="pack_copies",
    )(pos, held(sliced))


def heavy_project_kernel(
    pos, mine_ref, theirs_ref, r0, r1, r2, r3, router_ref, own_ref, other_ref, w_ref, *, depth, capacity
):
    side, core, y, xl = pos[1], pos[2], pos[3], pos[4]
    z_size = mine_ref.shape[0]
    for y_half in range(2):
        for x in range(2):
            for m in range(2):
                i = (y_half * 2 + x) * 2 + m
                for z in range(z_size):
                    base = ((y_half * 2 + x) * z_size + z) * 2
                    w_ref[m, pl.ds(pl.multiple_of((base + core) * depth, depth), depth), :] = mine_ref[
                        z, i * depth : (i + 1) * depth, :
                    ]
                    w_ref[m, pl.ds(pl.multiple_of((base + 1 - core) * depth, depth), depth), :] = theirs_ref[
                        z, i * depth : (i + 1) * depth, :
                    ]
    lane = lax.broadcasted_iota(jnp.int32, (capacity, 2 * HEAD_DIM), 1)
    keep = lane < HEAD_DIM
    upper = lane < HEAD_DIM + HEAD_DIM // 2
    own_w = w_ref[side]
    other_w = w_ref[1 - side]
    for d, piece in enumerate((r0, r1, r2, r3)):
        rows = piece[...].reshape(4 * capacity, piece.shape[2])
        for_other = jnp.dot(rows, other_w, preferred_element_type=jnp.float32)
        for_own = jnp.dot(rows, own_w, preferred_element_type=jnp.float32)
        score = jnp.dot(rows, router_ref[...], preferred_element_type=jnp.float32)
        high = score.astype(jnp.bfloat16).astype(jnp.float32)
        source_y = lax.rem(y - d + 4, 4)
        for which in range(2):
            source = source_y * 2 + (xl if which == 0 else 1 - xl)
            query = slice(which * 2 * capacity, which * 2 * capacity + capacity)
            keys = slice(query.stop, query.stop + capacity)
            at = pl.ds(pl.multiple_of(source * capacity, capacity), capacity)
            terms = jnp.where(upper, high[query], score[query] - high[query])
            left = jnp.where(keep, for_other[query, : 2 * HEAD_DIM], terms)
            other_ref[at, :] = jnp.concatenate([left, for_other[keys, 2 * HEAD_DIM :]], axis=1).astype(jnp.bfloat16)
            left = jnp.where(keep, for_own[query, : 2 * HEAD_DIM], score[query])
            own_ref[at, :] = jnp.concatenate([left, for_own[keys, 2 * HEAD_DIM :]], axis=1)


def heavy_project(pos, mine, theirs, pieces, router, depth):
    capacity = pieces[0].shape[1] // 2
    half = pieces[0].shape[2]
    slots = 8 * capacity
    return pl.pallas_call(
        functools.partial(heavy_project_kernel, depth=depth, capacity=capacity),
        out_shape=(
            pltpu.VMEM((slots, 4 * HEAD_DIM), jnp.float32),
            pltpu.VMEM((slots, 4 * HEAD_DIM), jnp.bfloat16),
        ),
        grid_spec=pltpu.PrefetchScalarGridSpec(
            num_scalar_prefetch=1,
            grid=(1,),
            in_specs=[HELD] * (3 + len(pieces)),
            out_specs=(HELD, HELD),
            scratch_shapes=[pltpu.VMEM((2, half, 4 * HEAD_DIM), jnp.bfloat16)],
        ),
        compiler_params=SMALL,
        name="heavy_project",
    )(pos, held(mine), held(theirs), *[held(p) for p in pieces], held(router))


def finish_kernel(pos, own_ref, arrived_ref, mine_ref, query_ref, gate_ref, copies_ref, *, capacity):
    own = own_ref[...]
    arrived = arrived_ref[...].astype(jnp.float32)
    total = (own + arrived).astype(jnp.bfloat16)
    lane = lax.broadcasted_iota(jnp.int32, (own.shape[0], 2 * HEAD_DIM), 1)
    query = total[:, : 2 * HEAD_DIM].astype(jnp.float32) * (HEAD_DIM ** -0.5)
    query_ref[...] = jnp.where(lane < HEAD_DIM, query, 0.0).astype(jnp.bfloat16)
    for t in range(copies_ref.shape[0]):
        copies_ref[t] = total[:, 2 * HEAD_DIM :]
    middle = HEAD_DIM + HEAD_DIM // 2
    logit = own[:, HEAD_DIM : HEAD_DIM + 1] + arrived[:, HEAD_DIM : HEAD_DIM + 1] + arrived[:, middle : middle + 1]
    gate = jnp.broadcast_to(1.0 / (1.0 + jnp.exp(-logit)), gate_ref.shape)
    group = own.shape[0] // capacity
    tail = mine_ref.shape[1] - group
    marks = mine_ref[pos[5], tail:, 2 * HEAD_DIM :].astype(jnp.float32)
    slot = lax.broadcasted_iota(jnp.int32, (capacity, 2 * HEAD_DIM), 0).astype(jnp.float32)
    for g in range(group):
        rows = slice(g * capacity, (g + 1) * capacity)
        gate_ref[rows, :] = jnp.where(slot < marks[g : g + 1, :], gate[rows], 0.0)


def finish(pos, own, arrived, mine, capacity):
    slots = own.shape[0]
    copies = mine.shape[0]
    return pl.pallas_call(
        functools.partial(finish_kernel, capacity=capacity),
        out_shape=(
            pltpu.VMEM((slots, 2 * HEAD_DIM), jnp.bfloat16),
            pltpu.VMEM((slots, 2 * HEAD_DIM), jnp.float32),
            pltpu.HBM((copies, slots, 2 * HEAD_DIM), jnp.bfloat16),
        ),
        grid_spec=pltpu.PrefetchScalarGridSpec(
            num_scalar_prefetch=1,
            grid=(1,),
            in_specs=[HELD, HELD, HELD],
            out_specs=(HELD, HELD, spec((copies, slots, 2 * HEAD_DIM), lambda i, p: (0, 0, 0))),
        ),
        compiler_params=SMALL,
        name="heavy_finish",
    )(pos, held(own), held(arrived), held(mine))


def out_weights_kernel(pos, mine_ref, theirs_ref, out_ref, bias_ref, *, depth, capacity):
    core = pos[2]
    z_size = mine_ref.shape[0]
    group = 8
    for i in range(group):
        for z in range(z_size):
            base = (i * z_size + z) * 2
            tile = slice(i * depth, (i + 1) * depth)
            out_ref[pl.ds(pl.multiple_of((base + core) * depth, depth), depth), :] = mine_ref[z, tile, : 2 * HEAD_DIM]
            out_ref[pl.ds(pl.multiple_of((base + 1 - core) * depth, depth), depth), :] = theirs_ref[
                z, tile, : 2 * HEAD_DIM
            ]
    lane = lax.broadcasted_iota(jnp.int32, (1, 2 * HEAD_DIM), 1)
    per_row = 2 * HEAD_DIM // capacity
    for which, ref in enumerate((mine_ref, theirs_ref)):
        for z in range(z_size):
            marks = ref[z, group * depth : group * depth + group, : 2 * HEAD_DIM].astype(jnp.float32)
            for part in range(group // per_row):
                count = jnp.zeros((1, 2 * HEAD_DIM), jnp.float32)
                for j in range(per_row):
                    g = part * per_row + j
                    count = jnp.where(lane // capacity == j, marks[g : g + 1, :], count)
                live = (lane % capacity).astype(jnp.float32) < count
                at = ((which * z_size + z_size - 1 - z) * (group // per_row) + part) * 2 * HEAD_DIM
                bias_ref[:, at : at + 2 * HEAD_DIM] = jnp.where(live, 0.0, NEG)


def out_weights(pos, mine, theirs, depth, capacity):
    z_size = mine.shape[0]
    return pl.pallas_call(
        functools.partial(out_weights_kernel, depth=depth, capacity=capacity),
        out_shape=(
            pltpu.VMEM((16 * z_size * depth, 2 * HEAD_DIM), jnp.bfloat16),
            pltpu.VMEM((1, 16 * z_size * capacity), jnp.float32),
        ),
        grid_spec=pltpu.PrefetchScalarGridSpec(
            num_scalar_prefetch=1,
            grid=(1,),
            in_specs=[HELD, HELD],
            out_specs=(HELD, HELD),
        ),
        compiler_params=SMALL,
        name="out_weights",
    )(pos, held(mine), held(theirs))


def heavy_first_kernel(q_ref, own_ref, bias_ref, sum_ref, peak_ref):
    keys = own_ref.shape[0]
    lane = lax.broadcasted_iota(jnp.int32, sum_ref.shape, 1)
    scores = lax.dot_general(q_ref[...], own_ref[...], NT, preferred_element_type=jnp.float32) + bias_ref[:, :keys]
    peak = jnp.max(scores, axis=1, keepdims=True)
    weights = jnp.exp(scores - peak)
    total = jnp.sum(weights, axis=1, keepdims=True)
    blended = jnp.dot(weights.astype(jnp.bfloat16), own_ref[...], preferred_element_type=jnp.float32)
    sum_ref[...] = jnp.where(lane < HEAD_DIM, total, blended)
    peak_ref[...] = jnp.broadcast_to(peak, peak_ref.shape)


def heavy_first(q, own, bias):
    shape = pltpu.VMEM(q.shape, jnp.float32)
    return pl.pallas_call(
        heavy_first_kernel,
        out_shape=(shape, shape),
        in_specs=[HELD] * 3,
        out_specs=(HELD, HELD),
        compiler_params=SMALL,
        name="heavy_first",
    )(*[held(a) for a in (q, own, bias)])


def heavy_kernel(q_ref, sum_ref, peak_ref, other_ref, bias_ref, w_ref, gate_ref, out_ref):
    keys = other_ref.shape[0]
    lane = lax.broadcasted_iota(jnp.int32, sum_ref.shape, 1)
    low = lane < HEAD_DIM
    scores = lax.dot_general(q_ref[...], other_ref[...], NT, preferred_element_type=jnp.float32) + bias_ref[:, keys:]
    before = peak_ref[:, 0:1]
    peak = jnp.maximum(before, jnp.max(scores, axis=1, keepdims=True))
    weights = jnp.exp(scores - peak)
    total = jnp.sum(weights, axis=1, keepdims=True)
    blended = jnp.dot(weights.astype(jnp.bfloat16), other_ref[...], preferred_element_type=jnp.float32)
    merged = sum_ref[...] * jnp.exp(before - peak) + jnp.where(low, total, blended)
    context = jnp.where(low, 0.0, merged / merged[:, 0:1]).astype(jnp.bfloat16)
    part = lax.dot_general(context, w_ref[...], NT, preferred_element_type=jnp.float32)
    part = (part * gate_ref[:, 0:1]).astype(jnp.bfloat16)
    count, capacity, half = out_ref.shape
    for i in range(count):
        top = i // 2 * capacity
        out_ref[i] = part[top : top + capacity, i % 2 * half : (i % 2 + 1) * half]


def heavy_attention(q, first, other, bias, w, gate, group):
    return pl.pallas_call(
        heavy_kernel,
        out_shape=jax.ShapeDtypeStruct((2 * group, q.shape[0] // group, w.shape[0] // 2), jnp.bfloat16),
        in_specs=[HELD] * 7,
        compiler_params=SMALL,
        name="heavy_attention",
    )(*[held(a) for a in (q, *first, other, bias, w, gate)])


def combine_kernel(own_ref, parts_ref, slots_ref, out_ref, hi_ref, lo_ref):
    step = pl.program_id(0)
    block = out_ref.shape[0]

    @pl.when(step == 0)
    def _():
        total = parts_ref[0].astype(jnp.float32)
        for i in range(1, parts_ref.shape[0]):
            total = total + parts_ref[i].astype(jnp.float32)
        hi = total.astype(jnp.bfloat16)
        hi_ref[...] = hi
        lo_ref[...] = (total - hi.astype(jnp.float32)).astype(jnp.bfloat16)

    capacity = slots_ref.shape[1]
    token = lax.broadcasted_iota(jnp.int32, (block, capacity), 0) + step * block
    pick = jnp.where(token == slots_ref[...], 1.0, 0.0).astype(jnp.bfloat16)
    heavy = jnp.dot(pick, hi_ref[...], preferred_element_type=jnp.float32)
    heavy = heavy + jnp.dot(pick, lo_ref[...], preferred_element_type=jnp.float32)
    out_ref[...] = (own_ref[...] + heavy).astype(jnp.bfloat16)


def combine(own, parts, slots):
    rows, cols = own.shape
    capacity = slots.shape[1]
    block = 128
    return pl.pallas_call(
        combine_kernel,
        out_shape=jax.ShapeDtypeStruct((rows, cols), jnp.bfloat16),
        grid=(rows // block,),
        in_specs=[spec((block, cols), lambda b: (b, 0)), HELD, spec((1, capacity), lambda b: (0, 0))],
        out_specs=spec((block, cols), lambda b: (b, 0)),
        scratch_shapes=[
            pltpu.VMEM((capacity, cols), jnp.bfloat16),
            pltpu.VMEM((capacity, cols), jnp.bfloat16),
        ],
        compiler_params=SMALL,
        name="combine",
    )(own, held(parts), slots)


def swap(a, axis):
    return lax.ppermute(a, axis, [(0, 1), (1, 0)])


def layer(
    normed,
    router,
    light_qkv,
    light_out,
    heavy_qkv,
    heavy_out,
    query_slots,
    query_count,
    key_slots,
    key_count,
):
    rows, half = normed.shape
    side = lax.axis_index("xh")
    core = lax.axis_index("c")
    shard_index = lax.axis_index(SEQ)
    shard_total = lax.axis_size(SEQ)
    y_size, _, z_size, _ = (lax.axis_size(axis) for axis in SEQ)
    capacity = query_slots.shape[1]
    feature_rows = heavy_qkv.shape[1]
    heads = heavy_qkv.shape[2] // HEAD_DIM
    group = heads
    pos = jnp.stack([shard_index, side, core, lax.axis_index("y"), lax.axis_index("xl"), lax.axis_index("z")]).astype(jnp.int32)

    slots = jnp.concatenate([query_slots[0], key_slots[0]])
    pick = (slots[:, None] == jnp.arange(rows, dtype=jnp.int32)[None, :]).astype(jnp.bfloat16)
    routed = jnp.dot(pick, normed, preferred_element_type=jnp.float32).astype(jnp.bfloat16)
    partner = swap(routed, "xl")
    pair = jnp.stack([routed, partner])
    router_own = lax.dynamic_slice_in_dim(router, side * half, half, 0)
    router_own = jnp.broadcast_to(router_own[:, None], (half, 2 * HEAD_DIM))
    pieces = [pair]
    for d in range(1, y_size):
        pieces.append(lax.ppermute(pair, "y", [(i, (i + d) % y_size) for i in range(y_size)]))

    by_head = pack_heads(key_count, query_count, heavy_qkv, jnp.transpose(heavy_out))
    sliced = lax.all_to_all(by_head, GROUP + ("xh",), 0, 0)
    packed = pack_copies(pos, sliced, z_size)
    mine = lax.all_to_all(packed, "z", 0, 0)
    theirs = swap(mine, "c")
    out_all, bias = out_weights(pos, mine, theirs, feature_rows, capacity)

    part_own, part_other = heavy_project(pos, mine, theirs, pieces, router_own, feature_rows)
    arrived = swap(part_other, "xh")
    query, gate, copies = finish(pos, part_own, arrived, mine, capacity)
    keys_own = lax.all_to_all(copies, "z", 0, 0, axis_index_groups=[list(range(z_size))[::-1]])
    keys_other = swap(keys_own, "c")
    keys_own = keys_own.reshape(-1, 2 * HEAD_DIM)
    keys_other = keys_other.reshape(-1, 2 * HEAD_DIM)
    first = heavy_first(query, keys_own, bias)
    outputs = heavy_attention(query, first, keys_other, bias, out_all, gate, group)
    parts = lax.all_to_all(outputs, GROUP + ("xh",), 0, 0)

    features = swap(normed, "xh")
    partial = project_own(pos, normed, light_qkv)
    paired, to_inner, to_outer = project_keys(pos, features, light_qkv, partial)
    inner = swap(to_inner, "c")
    ends = range(1, shard_total - 1, 2)
    outer = lax.ppermute(to_outer, SEQ, [(i, i + 1) for i in ends] + [(i + 1, i) for i in ends])
    queries = project_queries(pos, normed, features, light_qkv)
    context = light_attention(pos, queries, paired, inner, outer, rows * shard_total)
    context_recv = swap(context, "xh")

    depth = light_out.shape[0] // 2
    cut = lax.dynamic_slice(light_out, (core * depth, (1 - side) * half), (depth, half))
    mine_w = lax.ppermute(cut, ("xl", "xh"), [(i, 3 - i) for i in range(4)])
    theirs_w = swap(mine_w, "c")
    own = light_product(pos, context, context_recv, light_out, mine_w, theirs_w)
    return combine(own, parts, query_slots)


def solution(mesh):
    fine = Mesh(mesh.devices.reshape(4, 2, 8, 2, 2), SEQ + ("xh",))
    in_specs = (
        P(SEQ, "xh"),
        P(),
        P(None, None, "xh"),
        P("xh", None),
        P(None, SEQ, "xh"),
        P("xh", SEQ),
        P(SEQ, None),
        P(SEQ),
        P(SEQ, None),
        P(SEQ),
    )
    return jax.shard_map(layer, mesh=fine, in_specs=in_specs, out_specs=P(SEQ, "xh"), check_vma=False)
```
